32 devices in a mesh: groups: 2 (over y), space: 4 (over z), tm: 2 (over x), freq: 2 (over core).
Axes of the slice: x: 2, y: 2, z: 4, core: 2. Of those that a mesh axis runs over, the one named last changes fastest.
Arguments:
- snapshots: float32 [16, 64, 16384], P(None, 'space', ('groups', 'tm')), parts along dimension 2, may hold values from -28 to 28, as said below
- weights: float32 [16384], P(('groups', 'tm', 'space')), parts along dimension 0, may hold values from 0.3 to 3
Outputs:
- modes: float32 [16, 2, 16, 16384], P('freq', None, None, ('groups', 'tm', 'space')), parts along dimension 3
- r_factor: float32 [4, 16, 16, 16], P('groups', 'freq'), parts along dimension 0
The draws below stay inside these ranges and needn't reach their ends.
There are 2 independent parts, one for each index of `groups`. The reference program is written for one: setup_inputs(seed, part) draws one part's arguments, and reference() takes and returns one part's arrays. A program takes and returns all parts, laid end to end along the dimension named above; each array names one. Nothing has to cross between parts.
Inputs may be any that keep to these rules, and one draw needn't show every extreme that they name: `snapshots`: velocity fluctuations of the jet.
All inputs are finite; a program needn't handle non-finite values.
Results may differ from the reference program's by a relative error of at most 0.00009.
Values sent between devices are 32-bit elements; how exact they have to be, the bound alone decides.
A program may use at most 64 MiB of HBM per device.

```python
import math
import jax
import jax.numpy as jnp
from jax import lax

NB = 16
SEGMENT_FRAMES = 64
NF = 16
M = 8192


def draw_snapshots(key, part):
    first_key = jax.random.fold_in(jax.random.fold_in(key, 11), 0)
    place = jnp.arange(M, dtype=jnp.float32) / M
    envelope = 3.0 ** place
    field = jnp.clip(jax.random.normal(first_key, (NB, SEGMENT_FRAMES, M), jnp.float32), -6.0, 6.0)
    return field * envelope[None, None, :]


def levels(rng, extent, cuts, smallest, largest):
    factor_of, own = 1.0, jax.random.fold_in(rng, 6)
    for dim, blocks in cuts:
        heights = jnp.exp(jax.random.uniform(jax.random.fold_in(own, dim), (blocks,), jnp.float32, smallest / len(cuts), largest / len(cuts)))
        factor_of = factor_of * jnp.repeat(heights, extent[dim] // blocks).reshape([-1 if axis == dim else 1 for axis in range(len(extent))])
    return factor_of


def setup_inputs(seed: int = 0, part: int = 0) -> dict:
    seeds = jax.random.split(jax.random.key(seed), 3)
    part_splits = jax.random.split(jax.random.fold_in(seeds[2], part), 3)
    return {
        "snapshots": draw_snapshots(jax.random.fold_in(jax.random.fold_in(seeds[2], part), 71), part),
        "weights": jnp.clip(jnp.exp(math.log(3.0) - 2.3025851 * jax.random.uniform(part_splits[1], (M,), jnp.float32) ** levels(part_splits[1], (M,), ((0, 8),), -0.2, 0.2)), 0.3, 3.0),
    }


epsilon = 1e-05

def dft_table(first_freq, how_many, initial_moment, elapsed_timespan):
    recorded_moments = initial_moment + jnp.arange(elapsed_timespan, dtype=jnp.int32)
    fourier_cycle_rate = first_freq + 1 + jnp.arange(how_many, dtype=jnp.int32)
    every_time = jnp.arange(SEGMENT_FRAMES, dtype=jnp.float32)
    tapers = 0.5 - 0.5 * jnp.cos(2.0 * jnp.pi * every_time / SEGMENT_FRAMES)
    norm_taper = jnp.sqrt(jnp.sum(tapers * tapers))
    segment_hann_weighting = 0.5 - 0.5 * jnp.cos(2.0 * jnp.pi * recorded_moments.astype(jnp.float32) / SEGMENT_FRAMES)
    weighted = segment_hann_weighting / norm_taper
    twiddle_angle_list = fourier_cycle_rate[:, None] * recorded_moments[None, :] % SEGMENT_FRAMES
    phases = 2.0 * jnp.pi * twiddle_angle_list.astype(jnp.float32) / SEGMENT_FRAMES
    paired = jnp.stack([jnp.cos(phases) * weighted[None, :], -jnp.sin(phases) * weighted[None, :]], axis=1)
    return paired.reshape(2 * how_many, elapsed_timespan)

def contract(left, right):
    return jnp.einsum('fbm,fcm->fbc', left, right, precision=lax.Precision.HIGHEST)

def gram_terms(spectra, weights):
    real_part = spectra[:, 0]
    imag_part = spectra[:, 1]
    weighted_re = real_part * weights
    weighted_im = imag_part * weights
    gram_re = contract(weighted_re, real_part) + contract(weighted_im, imag_part)
    gram_im = contract(weighted_re, imag_part) - contract(weighted_im, real_part)
    return jnp.stack([gram_re, gram_im])

def factor(gram):
    positions = jnp.arange(NB, dtype=jnp.int32)
    rows_re = []
    rows_im = []
    for i in range(NB):
        accum_re = gram[0][:, i, :]
        accum_im = gram[1][:, i, :]
        for p in range(i):
            left_re = rows_re[p][:, i][:, None]
            left_im = rows_im[p][:, i][:, None]
            accum_re = accum_re - (left_re * rows_re[p] + left_im * rows_im[p])
            accum_im = accum_im - (left_re * rows_im[p] - left_im * rows_re[p])
        pivot = jnp.sqrt(accum_re[:, i] + epsilon)
        beyond = (positions > i)[None, :]
        at_diag = (positions == i)[None, :]
        rows_re.append(jnp.where(beyond, accum_re / pivot[:, None], 0.0) + jnp.where(at_diag, pivot[:, None], 0.0))
        rows_im.append(jnp.where(beyond, accum_im / pivot[:, None], 0.0))
    upper_re = jnp.stack(rows_re, axis=1)
    upper_im = jnp.stack(rows_im, axis=1)
    inverse_re = [None] * NB
    inverse_im = [None] * NB
    for i in range(NB - 1, -1, -1):
        accum_re = jnp.broadcast_to(jnp.where(positions == i, 1.0, 0.0).astype(jnp.float32)[None, :], upper_re[:, 0, :].shape)
        accum_im = jnp.zeros_like(accum_re)
        for p in range(i + 1, NB):
            coef_re = upper_re[:, i, p][:, None]
            coef_im = upper_im[:, i, p][:, None]
            accum_re = accum_re - (coef_re * inverse_re[p] - coef_im * inverse_im[p])
            accum_im = accum_im - (coef_re * inverse_im[p] + coef_im * inverse_re[p])
        pivot = upper_re[:, i, i][:, None]
        inverse_re[i] = accum_re / pivot
        inverse_im[i] = accum_im / pivot
    return (upper_re, upper_im, jnp.stack(inverse_re, axis=1), jnp.stack(inverse_im, axis=1))

def apply_inverse(left, inverse):
    return jnp.einsum('fbm,fbc->fcm', left, inverse, precision=lax.Precision.HIGHEST)

def build_modes(spectra, inverse_re, inverse_im):
    real_part = spectra[:, 0]
    imag_part = spectra[:, 1]
    modes_re = apply_inverse(real_part, inverse_re) - apply_inverse(imag_part, inverse_im)
    modes_im = apply_inverse(real_part, inverse_im) + apply_inverse(imag_part, inverse_re)
    return jnp.stack([modes_re, modes_im], axis=1)

def reference(snapshots, weights):
    table = dft_table(0, NF, 0, SEGMENT_FRAMES)
    spectra = jnp.einsum('ft,btm->fbm', table, snapshots, precision=lax.Precision.HIGHEST)
    spectra = spectra.reshape(NF, 2, NB, M)
    gram = gram_terms(spectra, weights) / M
    upper_re, upper_im, inverse_re, inverse_im = factor(gram)
    modes = build_modes(spectra, inverse_re, inverse_im)
    return (modes, jnp.stack([upper_re, upper_im]))
```

```python
import functools

import jax
import jax.numpy as jnp
import numpy as np
from jax import lax
from jax.experimental import pallas as pl
from jax.experimental.pallas import tpu as pltpu
from jax.sharding import PartitionSpec as P

SEGMENT_FRAMES = 64
NF = 16
GROUP = 4

epsilon = 1e-05
MESH = pl.DeviceIdType.MESH
HIGHEST = lax.Precision.HIGHEST


def dft_table(half, senders, local_times):
    moments = np.arange(SEGMENT_FRAMES)
    hann = 0.5 - 0.5 * np.cos(2.0 * np.pi * moments / SEGMENT_FRAMES)
    taper = hann / np.sqrt(np.sum(hann * hann))
    angle = (np.arange(NF) + 1)[:, None] * moments[None, :] % SEGMENT_FRAMES
    phase = 2.0 * np.pi * angle / SEGMENT_FRAMES
    pair = np.stack([np.cos(phase) * taper, -np.sin(phase) * taper])
    pair = pair.reshape(2, NF // half, half, senders, local_times)
    full = np.einsum("rhfzt,bc->hrbfzct", pair, np.eye(GROUP))
    shape = (NF // half, 2 * GROUP * half, senders * GROUP * local_times)
    return full.reshape(shape).astype(np.float32)


def xor(a, d, bits):
    out = a
    for k in range(bits):
        if d >> k & 1:
            bit = lax.rem(lax.div(a, 1 << k), 2)
            out = out + (1 << k) - (2 << k) * bit
    return out


def peers_along(me, count):
    bits = count.bit_length() - 1
    if count == 1 << bits:
        order = sorted(range(1, count), key=lambda d: -(d.bit_length()))
        return [xor(me, d, bits) for d in order]
    return [lax.rem(me + d, count) for d in range(1, count)]


def spectra_kernel(
    exchange, space, tm, total, snap, weight, table, x_out, g_out,
    recv, spec, away, g_send, g_recv,
    s_send, s_recv, l_sem, p_send, p_recv, gs_sem, gr_sem,
):
    core = lax.axis_index("freq")
    z = lax.axis_index("space")
    other = 1 - core
    rows = recv.shape[3]
    chunks = recv.shape[1] // GROUP
    half = spec.shape[3]
    z_peers = peers_along(z, space)
    m = lax.axis_index("tm")
    m_peers = peers_along(m, tm)
    g_peers = [(m, p) for p in z_peers] + [(o, p) for o in m_peers for p in [*z_peers, z]]

    def cols(p):
        return pl.ds(pl.multiple_of((p * 2 + core) * rows, rows), rows)

    def blocks(q):
        return pl.ds(q * GROUP, GROUP)

    def local(q):
        if exchange:
            source, slot = snap.at[blocks(q), :, cols(z)], z
        else:
            source, slot = snap.at[blocks(q)], 0
        return pltpu.make_async_copy(source, recv.at[slot, blocks(q)], l_sem.at[q])

    def send(q, i):
        return pltpu.make_async_remote_copy(
            src_ref=snap.at[blocks(q), :, cols(z_peers[i])],
            dst_ref=recv.at[z, blocks(q)],
            send_sem=s_send.at[q, i],
            recv_sem=s_recv.at[q, z],
            device_id={"space": z_peers[i]},
            device_id_type=MESH,
        )

    def arrive(q, i):
        p = z_peers[i]
        return pltpu.make_async_remote_copy(
            src_ref=snap.at[blocks(q), :, cols(p)],
            dst_ref=recv.at[p, blocks(q)],
            send_sem=s_send.at[q, i],
            recv_sem=s_recv.at[q, p],
            device_id={"space": p},
            device_id_type=MESH,
        )

    def trade(q, row):
        return pltpu.make_async_remote_copy(
            src_ref=away.at[q],
            dst_ref=spec.at[row, :, blocks(q)],
            send_sem=p_send.at[q],
            recv_sem=p_recv.at[q],
            device_id={"freq": other},
            device_id_type=MESH,
        )

    def gram_copy(i, slot):
        o, p = g_peers[i]
        return pltpu.make_async_remote_copy(
            src_ref=g_send,
            dst_ref=g_recv.at[slot],
            send_sem=gs_sem.at[i],
            recv_sem=gr_sem.at[slot],
            device_id={"space": p, "tm": o},
            device_id_type=MESH,
        )

    barrier = pltpu.get_barrier_semaphore()
    pl.semaphore_signal(barrier, inc=1, device_id={"freq": other}, device_id_type=MESH)
    for o, p in g_peers:
        pl.semaphore_signal(
            barrier, inc=1, device_id={"space": p, "tm": o}, device_id_type=MESH
        )
    for q in range(chunks):
        local(q).start()
    pl.semaphore_wait(barrier, 1 + len(g_peers))

    hops = range(len(z_peers)) if exchange else range(0)
    for q in range(chunks):
        for i in hops:
            send(q, i).start()

    both = jnp.concatenate([table[core], table[other]], axis=0)
    for q in range(chunks):
        local(q).wait()
        for i in hops:
            arrive(q, i).wait_recv()
        flat = recv[:, q * GROUP : (q + 1) * GROUP].reshape(-1, rows)
        got = jnp.dot(both, flat, precision=HIGHEST, preferred_element_type=jnp.float32)
        got = got.reshape(2, 2, GROUP, half, rows)
        away[q] = got[1]
        trade(q, core).start()
        spec[core, :, q * GROUP : (q + 1) * GROUP] = got[0]

    def gram(c):
        one = spec[c].reshape(-1, rows)
        return lax.dot_general(
            one * weight[c], one, (((1,), (1,)), ((), ())),
            precision=HIGHEST, preferred_element_type=jnp.float32,
        )

    product = gram(core)
    for q in range(chunks):
        trade(q, other).wait_recv()
    product = product + gram(other)
    n = product.shape[0] // 2
    pair = (
        product[:n, :n] + product[n:, n:],
        product[:n, n:] - product[n:, :n],
    )
    shape = (n // half, half, n)
    same = lax.rem(lax.broadcasted_iota(jnp.int32, shape, 2), half) == (
        lax.broadcasted_iota(jnp.int32, shape, 1)
    )
    for r in range(2):
        g_send[r] = jnp.sum(jnp.where(same, pair[r].reshape(shape), 0.0), axis=1)
    mine = m * space + z
    for i in range(len(g_peers)):
        gram_copy(i, mine).start()
    g_recv[mine] = g_send[...]
    for c in range(2):
        x_out[:, c * rows : (c + 1) * rows] = spec[c].reshape(-1, rows)
    for q in range(chunks):
        trade(q, core).wait_send()
        for i in hops:
            send(q, i).wait_send()
    for i, (o, p) in enumerate(g_peers):
        gram_copy(i, o * space + p).wait_recv()
    for i in range(len(g_peers)):
        gram_copy(i, mine).wait_send()
    acc = g_recv[0]
    for s in range(1, space * tm):
        acc = acc + g_recv[s]
    g_out[...] = acc * (1.0 / total)


def modes_kernel(half, gram, x, modes, upper):
    nb, lanes = gram.shape[1], gram.shape[2]
    row = lax.broadcasted_iota(jnp.int32, (nb, lanes), 0)
    lane = lax.broadcasted_iota(jnp.int32, (nb, lanes), 1)
    col = lane // half
    which = lane % half

    def pick(a, index):
        return jnp.take_along_axis(a, index, axis=1, mode="promise_in_bounds")

    re = gram[0] + jnp.where(row == col, epsilon, 0.0)
    im = gram[1]
    diag = jnp.zeros_like(re)
    for p in range(nb):
        index = which + p * half
        cr, ci = pick(re, index), pick(im, index)
        diag = jnp.where(row == p, cr, diag)
        if p == nb - 1:
            break
        inv = 1.0 / cr[p : p + 1]
        mr, mi = cr * inv, ci * inv
        pr, pi = re[p : p + 1], im[p : p + 1]
        here = col == p
        nr = jnp.where(here, 0.0, re) - (
            mr * jnp.where(here[:1], 1.0, pr) - mi * jnp.where(here[:1], 0.0, pi)
        )
        ni = jnp.where(here, 0.0, im) - (
            mr * jnp.where(here[:1], 0.0, pi) + mi * jnp.where(here[:1], 1.0, pr)
        )
        re = jnp.where(row > p, nr, re)
        im = jnp.where(row > p, ni, im)
    pivot = jnp.sqrt(diag)
    scale = 1.0 / pivot
    re, im = re * scale, im * scale
    ur = jnp.where(col > row, re, jnp.where(col == row, pivot, 0.0))
    ui = jnp.where(col > row, im, 0.0)
    lr = jnp.where(col < row, re, jnp.where(col == row, scale, 0.0))
    li = jnp.where(col < row, im, 0.0)
    for f in range(half):
        index = (lane * half + f) % lanes
        upper[0, f] = pick(ur, index)[:, :nb]
        upper[1, f] = pick(ui, index)[:, :nb]
    parts = []
    for f in range(half):
        fr = jnp.where(which == f, lr, 0.0)
        fi = jnp.where(which == f, li, 0.0)
        parts.append(jnp.concatenate([fr, fi], axis=1))
        parts.append(jnp.concatenate([-fi, fr], axis=1))
    big = jnp.concatenate(parts, axis=0)
    out = jnp.dot(big, x[...], precision=HIGHEST, preferred_element_type=jnp.float32)
    modes[...] = out.reshape(modes.shape)


def on_device(snapshots, weights):
    freq = lax.axis_size("freq")
    space = lax.axis_size("space")
    tm = lax.axis_size("tm")
    assert freq == 2
    half = NF // freq
    nb, local_times, columns = snapshots.shape
    rows = columns // (space * freq)
    exchange = local_times % 8 == 0
    if not exchange:
        shaped = snapshots.reshape(nb, local_times, space, freq, rows)
        own = lax.dynamic_index_in_dim(shaped, lax.axis_index("freq"), 3, keepdims=False)
        pieces = lax.all_to_all(own, "space", split_axis=2, concat_axis=1, tiled=True)
        snapshots = pieces.reshape(nb, SEGMENT_FRAMES, rows)
    senders = space if exchange else 1
    times = SEGMENT_FRAMES // senders
    chunks = nb // GROUP
    table = jnp.asarray(dft_table(half, senders, times))
    weight = weights.reshape(freq, 1, rows)
    lanes = nb * half
    peers = space * tm
    vmem = pl.BlockSpec(memory_space=pltpu.VMEM)
    dma = pltpu.SemaphoreType.DMA
    x, gram = pl.pallas_call(
        functools.partial(
            spectra_kernel, exchange, space, tm, weights.shape[0] * space * tm
        ),
        out_shape=(
            jax.ShapeDtypeStruct((2 * lanes, freq * rows), jnp.float32),
            jax.ShapeDtypeStruct((2, nb, lanes), jnp.float32),
        ),
        in_specs=[pl.BlockSpec(memory_space=pl.ANY), vmem, vmem],
        out_specs=(vmem, vmem),
        scratch_shapes=[
            pltpu.VMEM((senders, nb, times, rows), jnp.float32),
            pltpu.VMEM((freq, 2, nb, half, rows), jnp.float32),
            pltpu.VMEM((chunks, 2, GROUP, half, rows), jnp.float32),
            pltpu.VMEM((2, nb, lanes), jnp.float32),
            pltpu.VMEM((peers, 2, nb, lanes), jnp.float32),
            dma((chunks, max(space - 1, 1))),
            dma((chunks, space)),
            dma((chunks,)),
            dma((chunks,)),
            dma((chunks,)),
            dma((peers,)),
            dma((peers,)),
        ],
        compiler_params=pltpu.CompilerParams(
            collective_id=0, has_side_effects=True, vmem_limit_bytes=40 * 2**20
        ),
        name="spectra",
    )(snapshots, weight, table)
    modes, upper = pl.pallas_call(
        functools.partial(modes_kernel, half),
        out_shape=(
            jax.ShapeDtypeStruct((half, 2, nb, freq * rows), jnp.float32),
            jax.ShapeDtypeStruct((2, half, nb, nb), jnp.float32),
        ),
        in_specs=[vmem, vmem],
        out_specs=(vmem, vmem),
        compiler_params=pltpu.CompilerParams(vmem_limit_bytes=40 * 2**20),
        name="modes",
    )(gram, x)
    return modes, upper


def solution(mesh):
    return jax.shard_map(
        on_device,
        mesh=mesh,
        in_specs=(P(None, "space", ("groups", "tm")), P(("groups", "tm", "space"))),
        out_specs=(
            P("freq", None, None, ("groups", "tm", "space")),
            P("groups", "freq", None, None),
        ),
        check_vma=False,
    )
```

```python
import functools

import jax
import jax.numpy as jnp
import numpy as np
from jax import lax
from jax.experimental import pallas as pl
from jax.experimental.pallas import tpu as pltpu
from jax.sharding import PartitionSpec as P

SEGMENT_FRAMES = 64
NF = 16
GROUP = 4

epsilon = 1e-05
MESH = pl.DeviceIdType.MESH
HIGHEST = lax.Precision.HIGHEST


def dft_table(half, senders, local_times):
    moments = np.arange(SEGMENT_FRAMES)
    hann = 0.5 - 0.5 * np.cos(2.0 * np.pi * moments / SEGMENT_FRAMES)
    taper = hann / np.sqrt(np.sum(hann * hann))
    angle = (np.arange(NF) + 1)[:, None] * moments[None, :] % SEGMENT_FRAMES
    phase = 2.0 * np.pi * angle / SEGMENT_FRAMES
    pair = np.stack([np.cos(phase) * taper, -np.sin(phase) * taper])
    pair = pair.reshape(2, NF // half, half, senders, local_times)
    full = np.einsum("rhfzt,bc->hrbfzct", pair, np.eye(GROUP))
    shape = (NF // half, 2 * GROUP * half, senders * GROUP * local_times)
    return full.reshape(shape).astype(np.float32)


def xor(a, d, bits):
    out = 0
    for k in range(bits):
        first = lax.rem(lax.div(a, 1 << k), 2)
        second = lax.rem(lax.div(d, 1 << k), 2)
        out = out + (1 << k) * (first + second - 2 * first * second)
    return out


def peers_along(me, count, late):
    bits = count.bit_length() - 1
    if count != 1 << bits:
        return [lax.rem(me + d, count) for d in range(1, count)]
    near = list(range(1, count // 2))
    far = list(range(count // 2, count))
    early, after = far + near, near + far
    return [
        xor(me, a + late * (b - a), bits) for a, b in zip(early, after)
    ]


def spectra_kernel(
    exchange, space, tm, total, snap, weight_in, table_in, x_out, g_out,
    weight, table, recv, spec, away, g_send, g_recv,
    c_sem, s_send, s_recv, l_sem, p_send, p_recv, gs_sem, gr_sem,
):
    core = lax.axis_index("freq")
    z = lax.axis_index("space")
    other = 1 - core
    rows = recv.shape[3]
    chunks = recv.shape[1] // GROUP
    half = spec.shape[3]
    z_peers = peers_along(z, space, 0)
    m = lax.axis_index("tm")
    m_peers = peers_along(m, tm, 0)
    g_peers = [(m, p) for p in z_peers] + [(o, p) for o in m_peers for p in [*z_peers, z]]

    def cols(p):
        return pl.ds(pl.multiple_of((p * 2 + core) * rows, rows), rows)

    def blocks(q):
        return pl.ds(q * GROUP, GROUP)

    def local(q):
        if exchange:
            source, slot = snap.at[blocks(q), :, cols(z)], z
        else:
            source, slot = snap.at[blocks(q)], 0
        return pltpu.make_async_copy(source, recv.at[slot, blocks(q)], l_sem.at[q])

    def send(q, i):
        return pltpu.make_async_remote_copy(
            src_ref=snap.at[blocks(q), :, cols(z_peers[i])],
            dst_ref=recv.at[z, blocks(q)],
            send_sem=s_send.at[q, i],
            recv_sem=s_recv.at[q, z],
            device_id={"space": z_peers[i]},
            device_id_type=MESH,
        )

    def arrive(q, i):
        p = z_peers[i]
        return pltpu.make_async_remote_copy(
            src_ref=snap.at[blocks(q), :, cols(p)],
            dst_ref=recv.at[p, blocks(q)],
            send_sem=s_send.at[q, i],
            recv_sem=s_recv.at[q, p],
            device_id={"space": p},
            device_id_type=MESH,
        )

    def trade(q, row):
        return pltpu.make_async_remote_copy(
            src_ref=away.at[q],
            dst_ref=spec.at[row, :, blocks(q)],
            send_sem=p_send.at[q],
            recv_sem=p_recv.at[q],
            device_id={"freq": other},
            device_id_type=MESH,
        )

    def gram_copy(i, slot):
        o, p = g_peers[i]
        return pltpu.make_async_remote_copy(
            src_ref=g_send,
            dst_ref=g_recv.at[slot],
            send_sem=gs_sem.at[i],
            recv_sem=gr_sem.at[slot],
            device_id={"space": p, "tm": o},
            device_id_type=MESH,
        )

    barrier = pltpu.get_barrier_semaphore()
    pl.semaphore_signal(barrier, inc=1, device_id={"freq": other}, device_id_type=MESH)
    for o, p in g_peers:
        pl.semaphore_signal(
            barrier, inc=1, device_id={"space": p, "tm": o}, device_id_type=MESH
        )
    constants = [
        pltpu.make_async_copy(weight_in, weight, c_sem.at[0]),
        pltpu.make_async_copy(table_in, table, c_sem.at[1]),
    ]
    for copy in constants:
        copy.start()
    pl.semaphore_wait(barrier, 1 + len(g_peers))

    hops = range(len(z_peers)) if exchange else range(0)
    for q in range(chunks):
        for i in hops:
            send(q, i).start()
    for q in range(chunks):
        local(q).start()

    for copy in constants:
        copy.wait()
    both = jnp.concatenate([table[core], table[other]], axis=0)
    for q in range(chunks):
        local(q).wait()
        for i in hops:
            arrive(q, i).wait_recv()
        flat = recv[:, q * GROUP : (q + 1) * GROUP].reshape(-1, rows)
        got = jnp.dot(both, flat, precision=HIGHEST, preferred_element_type=jnp.float32)
        got = got.reshape(2, 2, GROUP, half, rows)
        away[q] = got[1]
        trade(q, core).start()
        spec[core, :, q * GROUP : (q + 1) * GROUP] = got[0]

    def gram(c):
        one = spec[c].reshape(-1, rows)
        return lax.dot_general(
            one * weight[c], one, (((1,), (1,)), ((), ())),
            precision=HIGHEST, preferred_element_type=jnp.float32,
        )

    product = gram(core)
    for q in range(chunks):
        trade(q, other).wait_recv()
    product = product + gram(other)
    n = product.shape[0] // 2
    pair = (
        product[:n, :n] + product[n:, n:],
        product[:n, n:] - product[n:, :n],
    )
    shape = (n // half, half, n)
    same = lax.rem(lax.broadcasted_iota(jnp.int32, shape, 2), half) == (
        lax.broadcasted_iota(jnp.int32, shape, 1)
    )
    for r in range(2):
        g_send[r] = jnp.sum(jnp.where(same, pair[r].reshape(shape), 0.0), axis=1)
    mine = m * space + z
    for i in range(len(g_peers)):
        gram_copy(i, mine).start()
    g_recv[mine] = g_send[...]
    for c in range(2):
        x_out[:, c * rows : (c + 1) * rows] = spec[c].reshape(-1, rows)
    for q in range(chunks):
        trade(q, core).wait_send()
        for i in hops:
            send(q, i).wait_send()
    for i, (o, p) in enumerate(g_peers):
        gram_copy(i, o * space + p).wait_recv()
    for i in range(len(g_peers)):
        gram_copy(i, mine).wait_send()
    acc = g_recv[0]
    for s in range(1, space * tm):
        acc = acc + g_recv[s]
    g_out[...] = acc * (1.0 / total)


def modes_kernel(half, gram, x, modes, upper):
    nb, lanes = gram.shape[1], gram.shape[2]
    row = lax.broadcasted_iota(jnp.int32, (nb, lanes), 0)
    lane = lax.broadcasted_iota(jnp.int32, (nb, lanes), 1)
    col = lane // half
    which = lane % half

    def pick(a, index):
        return jnp.take_along_axis(a, index, axis=1, mode="promise_in_bounds")

    re = gram[0] + jnp.where(row == col, epsilon, 0.0)
    im = gram[1]
    diag = jnp.zeros_like(re)
    for p in range(nb):
        index = which + p * half
        cr, ci = pick(re, index), pick(im, index)
        diag = jnp.where(row == p, cr, diag)
        if p == nb - 1:
            break
        inv = 1.0 / cr[p : p + 1]
        mr, mi = cr * inv, ci * inv
        pr, pi = re[p : p + 1], im[p : p + 1]
        here = col == p
        nr = jnp.where(here, 0.0, re) - (
            mr * jnp.where(here[:1], 1.0, pr) - mi * jnp.where(here[:1], 0.0, pi)
        )
        ni = jnp.where(here, 0.0, im) - (
            mr * jnp.where(here[:1], 0.0, pi) + mi * jnp.where(here[:1], 1.0, pr)
        )
        re = jnp.where(row > p, nr, re)
        im = jnp.where(row > p, ni, im)
    pivot = jnp.sqrt(diag)
    scale = 1.0 / pivot
    re, im = re * scale, im * scale
    ur = jnp.where(col > row, re, jnp.where(col == row, pivot, 0.0))
    ui = jnp.where(col > row, im, 0.0)
    lr = jnp.where(col < row, re, jnp.where(col == row, scale, 0.0))
    li = jnp.where(col < row, im, 0.0)
    for f in range(half):
        index = (lane * half + f) % lanes
        upper[0, f] = pick(ur, index)[:, :nb]
        upper[1, f] = pick(ui, index)[:, :nb]
    parts = []
    for f in range(half):
        fr = jnp.where(which == f, lr, 0.0)
        fi = jnp.where(which == f, li, 0.0)
        parts.append(jnp.concatenate([fr, fi], axis=1))
        parts.append(jnp.concatenate([-fi, fr], axis=1))
    big = jnp.concatenate(parts, axis=0)
    out = jnp.dot(big, x[...], precision=HIGHEST, preferred_element_type=jnp.float32)
    modes[...] = out.reshape(modes.shape)


def on_device(snapshots, weights):
    freq = lax.axis_size("freq")
    space = lax.axis_size("space")
    tm = lax.axis_size("tm")
    assert freq == 2
    half = NF // freq
    nb, local_times, columns = snapshots.shape
    rows = columns // (space * freq)
    exchange = local_times % 8 == 0
    if not exchange:
        shaped = snapshots.reshape(nb, local_times, space, freq, rows)
        own = lax.dynamic_index_in_dim(shaped, lax.axis_index("freq"), 3, keepdims=False)
        pieces = lax.all_to_all(own, "space", split_axis=2, concat_axis=1, tiled=True)
        snapshots = pieces.reshape(nb, SEGMENT_FRAMES, rows)
    senders = space if exchange else 1
    times = SEGMENT_FRAMES // senders
    chunks = nb // GROUP
    table = jnp.asarray(dft_table(half, senders, times))
    weight = weights.reshape(freq, 1, rows)
    lanes = nb * half
    peers = space * tm
    vmem = pl.BlockSpec(memory_space=pltpu.VMEM)
    dma = pltpu.SemaphoreType.DMA
    x, gram = pl.pallas_call(
        functools.partial(
            spectra_kernel, exchange, space, tm, weights.shape[0] * space * tm
        ),
        out_shape=(
            jax.ShapeDtypeStruct((2 * lanes, freq * rows), jnp.float32),
            jax.ShapeDtypeStruct((2, nb, lanes), jnp.float32),
        ),
        in_specs=[pl.BlockSpec(memory_space=pltpu.HBM)] * 3,
        out_specs=(vmem, vmem),
        scratch_shapes=[
            pltpu.VMEM(weight.shape, jnp.float32),
            pltpu.VMEM(table.shape, jnp.float32),
            pltpu.VMEM((senders, nb, times, rows), jnp.float32),
            pltpu.VMEM((freq, 2, nb, half, rows), jnp.float32),
            pltpu.VMEM((chunks, 2, GROUP, half, rows), jnp.float32),
            pltpu.VMEM((2, nb, lanes), jnp.float32),
            pltpu.VMEM((peers, 2, nb, lanes), jnp.float32),
            dma((2,)),
            dma((chunks, max(space - 1, 1))),
            dma((chunks, space)),
            dma((chunks,)),
            dma((chunks,)),
            dma((chunks,)),
            dma((peers,)),
            dma((peers,)),
        ],
        compiler_params=pltpu.CompilerParams(
            collective_id=0, has_side_effects=True, vmem_limit_bytes=52 * 2**20
        ),
        name="spectra",
    )(snapshots, weight, table)
    modes, upper = pl.pallas_call(
        functools.partial(modes_kernel, half),
        out_shape=(
            jax.ShapeDtypeStruct((half, 2, nb, freq * rows), jnp.float32),
            jax.ShapeDtypeStruct((2, half, nb, nb), jnp.float32),
        ),
        in_specs=[vmem, vmem],
        out_specs=(vmem, vmem),
        compiler_params=pltpu.CompilerParams(vmem_limit_bytes=40 * 2**20),
        name="modes",
    )(gram, x)
    return modes, upper


def solution(mesh):
    return jax.shard_map(
        on_device,
        mesh=mesh,
        in_specs=(P(None, "space", ("groups", "tm")), P(("groups", "tm", "space"))),
        out_specs=(
            P("freq", None, None, ("groups", "tm", "space")),
            P("groups", "freq", None, None),
        ),
        check_vma=False,
    )
```

```python
import functools

import jax
import jax.numpy as jnp
import numpy as np
from jax import lax
from jax.experimental import pallas as pl
from jax.experimental.pallas import tpu as pltpu
from jax.sharding import PartitionSpec as P

SEGMENT_FRAMES = 64
NF = 16
GROUP = 4

epsilon = 1e-05
MESH = pl.DeviceIdType.MESH
HIGHEST = lax.Precision.HIGHEST


def dft_table(half, senders, local_times):
    moments = np.arange(SEGMENT_FRAMES)
    hann = 0.5 - 0.5 * np.cos(2.0 * np.pi * moments / SEGMENT_FRAMES)
    taper = hann / np.sqrt(np.sum(hann * hann))
    angle = (np.arange(NF) + 1)[:, None] * moments[None, :] % SEGMENT_FRAMES
    phase = 2.0 * np.pi * angle / SEGMENT_FRAMES
    pair = np.stack([np.cos(phase) * taper, -np.sin(phase) * taper])
    pair = pair.reshape(2, NF // half, half, senders, local_times)
    full = np.einsum("rhfzt,bc->hrbfzct", pair, np.eye(GROUP))
    shape = (NF // half, 2 * GROUP * half, senders * GROUP * local_times)
    return full.reshape(shape).astype(np.float32)


def xor(a, d, bits):
    out = 0
    for k in range(bits):
        first = lax.rem(lax.div(a, 1 << k), 2)
        second = lax.rem(lax.div(d, 1 << k), 2)
        out = out + (1 << k) * (first + second - 2 * first * second)
    return out


def peers_along(me, count, late):
    bits = count.bit_length() - 1
    if count != 1 << bits:
        return [lax.rem(me + d, count) for d in range(1, count)]
    near = list(range(1, count // 2))
    far = list(range(count // 2, count))
    early, after = far + near, near + far
    return [
        xor(me, a + late * (b - a), bits) for a, b in zip(early, after)
    ]


def spectra_kernel(
    exchange, space, tm, total, snap, weight_in, table_in, x_out, g_out,
    weight, table, recv, spec, away, g_send, g_recv,
    c_sem, s_send, s_recv, l_sem, p_send, p_recv, gs_sem, gr_sem,
):
    core = lax.axis_index("freq")
    z = lax.axis_index("space")
    other = 1 - core
    rows = recv.shape[3]
    chunks = recv.shape[1] // GROUP
    half = spec.shape[3]
    z_peers = peers_along(z, space, 0)
    m = lax.axis_index("tm")
    m_peers = peers_along(m, tm, 0)
    g_peers = [(m, p) for p in z_peers] + [(o, p) for o in m_peers for p in [*z_peers, z]]

    def cols(p):
        return pl.ds(pl.multiple_of((p * 2 + core) * rows, rows), rows)

    def blocks(q):
        return pl.ds(q * GROUP, GROUP)

    def local(q):
        if exchange:
            source, slot = snap.at[blocks(q), :, cols(z)], z
        else:
            source, slot = snap.at[blocks(q)], 0
        return pltpu.make_async_copy(source, recv.at[slot, blocks(q)], l_sem.at[q])

    def send(q, i):
        return pltpu.make_async_remote_copy(
            src_ref=snap.at[blocks(q), :, cols(z_peers[i])],
            dst_ref=recv.at[z, blocks(q)],
            send_sem=s_send.at[q, i],
            recv_sem=s_recv.at[q, z],
            device_id={"space": z_peers[i]},
            device_id_type=MESH,
        )

    def arrive(q, i):
        p = z_peers[i]
        return pltpu.make_async_remote_copy(
            src_ref=snap.at[blocks(q), :, cols(p)],
            dst_ref=recv.at[p, blocks(q)],
            send_sem=s_send.at[q, i],
            recv_sem=s_recv.at[q, p],
            device_id={"space": p},
            device_id_type=MESH,
        )

    def trade(q, row):
        return pltpu.make_async_remote_copy(
            src_ref=away.at[q],
            dst_ref=spec.at[row, :, blocks(q)],
            send_sem=p_send.at[q],
            recv_sem=p_recv.at[q],
            device_id={"freq": other},
            device_id_type=MESH,
        )

    def gram_copy(i, slot):
        o, p = g_peers[i]
        return pltpu.make_async_remote_copy(
            src_ref=g_send,
            dst_ref=g_recv.at[slot],
            send_sem=gs_sem.at[i],
            recv_sem=gr_sem.at[slot],
            device_id={"space": p, "tm": o},
            device_id_type=MESH,
        )

    barrier = pltpu.get_barrier_semaphore()
    pl.semaphore_signal(barrier, inc=1, device_id={"freq": other}, device_id_type=MESH)
    for o, p in g_peers:
        pl.semaphore_signal(
            barrier, inc=1, device_id={"space": p, "tm": o}, device_id_type=MESH
        )
    constants = [
        pltpu.make_async_copy(weight_in, weight, c_sem.at[0]),
        pltpu.make_async_copy(table_in, table, c_sem.at[1]),
    ]
    for copy in constants:
        copy.start()
    pl.semaphore_wait(barrier, 1 + len(g_peers))

    hops = range(len(z_peers)) if exchange else range(0)
    for q in range(chunks):
        for i in hops:
            send(q, i).start()
    for q in range(chunks):
        local(q).start()

    for copy in constants:
        copy.wait()
    both = jnp.concatenate([table[core], table[other]], axis=0)
    for q in range(chunks):
        local(q).wait()
        for i in hops:
            arrive(q, i).wait_recv()
        flat = recv[:, q * GROUP : (q + 1) * GROUP].reshape(-1, rows)
        got = jnp.dot(both, flat, precision=HIGHEST, preferred_element_type=jnp.float32)
        got = got.reshape(2, 2, GROUP, half, rows)
        away[q] = got[1]
        trade(q, core).start()
        spec[core, :, q * GROUP : (q + 1) * GROUP] = got[0]

    def gram(c):
        one = spec[c].reshape(-1, rows)
        return lax.dot_general(
            one * weight[c], one, (((1,), (1,)), ((), ())),
            precision=HIGHEST, preferred_element_type=jnp.float32,
        )

    product = gram(core)
    for q in range(chunks):
        trade(q, other).wait_recv()
    product = product + gram(other)
    n = product.shape[0] // 2
    pair = (
        product[:n, :n] + product[n:, n:],
        product[:n, n:] - product[n:, :n],
    )
    shape = (n // half, half, n)
    same = lax.rem(lax.broadcasted_iota(jnp.int32, shape, 2), half) == (
        lax.broadcasted_iota(jnp.int32, shape, 1)
    )
    for r in range(2):
        g_send[r] = jnp.sum(jnp.where(same, pair[r].reshape(shape), 0.0), axis=1)
    mine = m * space + z
    for i in range(len(g_peers)):
        gram_copy(i, mine).start()
    g_recv[mine] = g_send[...]
    for c in range(2):
        x_out[:, c * rows : (c + 1) * rows] = spec[c].reshape(-1, rows)
    for q in range(chunks):
        trade(q, core).wait_send()
        for i in hops:
            send(q, i).wait_send()
    for i, (o, p) in enumerate(g_peers):
        gram_copy(i, o * space + p).wait_recv()
    for i in range(len(g_peers)):
        gram_copy(i, mine).wait_send()
    acc = g_recv[0]
    for s in range(1, space * tm):
        acc = acc + g_recv[s]
    g_out[...] = acc * (1.0 / total)


def factor(half, gram, upper, big):
    nb, lanes = gram.shape[1], gram.shape[2]
    row = lax.broadcasted_iota(jnp.int32, (nb, lanes), 0)
    lane = lax.broadcasted_iota(jnp.int32, (nb, lanes), 1)
    col = lane // half
    which = lane % half

    def pick(a, index):
        return jnp.take_along_axis(a, index, axis=1, mode="promise_in_bounds")

    re = gram[0] + jnp.where(row == col, epsilon, 0.0)
    im = gram[1]
    diag = jnp.zeros_like(re)
    for p in range(nb):
        index = which + p * half
        cr, ci = pick(re, index), pick(im, index)
        diag = jnp.where(row == p, cr, diag)
        if p == nb - 1:
            break
        inv = 1.0 / cr[p : p + 1]
        mr, mi = cr * inv, ci * inv
        pr, pi = re[p : p + 1], im[p : p + 1]
        here = col == p
        nr = jnp.where(here, 0.0, re) - (
            mr * jnp.where(here[:1], 1.0, pr) - mi * jnp.where(here[:1], 0.0, pi)
        )
        ni = jnp.where(here, 0.0, im) - (
            mr * jnp.where(here[:1], 0.0, pi) + mi * jnp.where(here[:1], 1.0, pr)
        )
        re = jnp.where(row > p, nr, re)
        im = jnp.where(row > p, ni, im)
    pivot = jnp.sqrt(diag)
    scale = 1.0 / pivot
    re, im = re * scale, im * scale
    ur = jnp.where(col > row, re, jnp.where(col == row, pivot, 0.0))
    ui = jnp.where(col > row, im, 0.0)
    lr = jnp.where(col < row, re, jnp.where(col == row, scale, 0.0))
    li = jnp.where(col < row, im, 0.0)
    for f in range(half):
        index = (lane * half + f) % lanes
        upper[0, f] = pick(ur, index)[:, :nb]
        upper[1, f] = pick(ui, index)[:, :nb]
    parts = []
    for f in range(half):
        fr = jnp.where(which == f, lr, 0.0)
        fi = jnp.where(which == f, li, 0.0)
        parts.append(jnp.concatenate([fr, fi], axis=1))
        parts.append(jnp.concatenate([-fi, fr], axis=1))
    big[...] = jnp.concatenate(parts, axis=0)


def modes_kernel(half, gram, x, modes, upper, big):
    @pl.when(pl.program_id(0) == 0)
    def _():
        factor(half, gram, upper, big)

    out = jnp.dot(big[...], x[...], precision=HIGHEST, preferred_element_type=jnp.float32)
    modes[...] = out.reshape(modes.shape)


def on_device(snapshots, weights):
    freq = lax.axis_size("freq")
    space = lax.axis_size("space")
    tm = lax.axis_size("tm")
    assert freq == 2
    half = NF // freq
    nb, local_times, columns = snapshots.shape
    rows = columns // (space * freq)
    exchange = local_times % 8 == 0
    if not exchange:
        shaped = snapshots.reshape(nb, local_times, space, freq, rows)
        own = lax.dynamic_index_in_dim(shaped, lax.axis_index("freq"), 3, keepdims=False)
        pieces = lax.all_to_all(own, "space", split_axis=2, concat_axis=1, tiled=True)
        snapshots = pieces.reshape(nb, SEGMENT_FRAMES, rows)
    senders = space if exchange else 1
    times = SEGMENT_FRAMES // senders
    chunks = nb // GROUP
    table = jnp.asarray(dft_table(half, senders, times))
    weight = weights.reshape(freq, 1, rows)
    lanes = nb * half
    peers = space * tm
    vmem = pl.BlockSpec(memory_space=pltpu.VMEM)
    dma = pltpu.SemaphoreType.DMA
    x, gram = pl.pallas_call(
        functools.partial(
            spectra_kernel, exchange, space, tm, weights.shape[0] * space * tm
        ),
        out_shape=(
            jax.ShapeDtypeStruct((2 * lanes, freq * rows), jnp.float32),
            jax.ShapeDtypeStruct((2, nb, lanes), jnp.float32),
        ),
        in_specs=[pl.BlockSpec(memory_space=pltpu.HBM)] * 3,
        out_specs=(vmem, vmem),
        scratch_shapes=[
            pltpu.VMEM(weight.shape, jnp.float32),
            pltpu.VMEM(table.shape, jnp.float32),
            pltpu.VMEM((senders, nb, times, rows), jnp.float32),
            pltpu.VMEM((freq, 2, nb, half, rows), jnp.float32),
            pltpu.VMEM((chunks, 2, GROUP, half, rows), jnp.float32),
            pltpu.VMEM((2, nb, lanes), jnp.float32),
            pltpu.VMEM((peers, 2, nb, lanes), jnp.float32),
            dma((2,)),
            dma((chunks, max(space - 1, 1))),
            dma((chunks, space)),
            dma((chunks,)),
            dma((chunks,)),
            dma((chunks,)),
            dma((peers,)),
            dma((peers,)),
        ],
        compiler_params=pltpu.CompilerParams(
            collective_id=0, has_side_effects=True, vmem_limit_bytes=52 * 2**20
        ),
        name="spectra",
    )(snapshots, weight, table)
    modes, upper = pl.pallas_call(
        functools.partial(modes_kernel, half),
        out_shape=(
            jax.ShapeDtypeStruct((half, 2, nb, freq * rows), jnp.float32),
            jax.ShapeDtypeStruct((2, half, nb, nb), jnp.float32),
        ),
        grid=(2,),
        in_specs=[
            pl.BlockSpec((2, nb, lanes), lambda j: (0, 0, 0)),
            pl.BlockSpec((2 * lanes, rows), lambda j: (0, j)),
        ],
        out_specs=(
            pl.BlockSpec((half, 2, nb, rows), lambda j: (0, 0, 0, j)),
            pl.BlockSpec((2, half, nb, nb), lambda j: (0, 0, 0, 0)),
        ),
        scratch_shapes=[pltpu.VMEM((2 * lanes, 2 * lanes), jnp.float32)],
        compiler_params=pltpu.CompilerParams(vmem_limit_bytes=40 * 2**20),
        name="modes",
    )(gram, x)
    return modes, upper


def solution(mesh):
    return jax.shard_map(
        on_device,
        mesh=mesh,
        in_specs=(P(None, "space", ("groups", "tm")), P(("groups", "tm", "space"))),
        out_specs=(
            P("freq", None, None, ("groups", "tm", "space")),
            P("groups", "freq", None, None),
        ),
        check_vma=False,
    )
```
